512 devices in a mesh: aux: 16 (over z_hi, y, core), occ: 32 (over x, z_lo).
Axes of the slice: x: 4, y: 4, z: 16 (z_hi: 2, z_lo: 8; z = z_hi * 8 + z_lo), core: 2. Of those that a mesh axis runs over, the one named last changes fastest.
Arguments:
- half_ints: bfloat16 [1024, 512, 1024], P('aux', 'occ'), may hold values from -0.71875 to 0.71875
- orbitals: bfloat16 [1024, 512], replicated, may hold values from -0.1875 to 0.1875
- eps_occ: float32 [512], replicated, may hold values from -1.5 to -0.3
- eps_vir: float32 [512], replicated, may hold values from 0.3 to 2.5
Outputs:
- density: bfloat16 [1024, 512, 512], P('aux', 'occ')
The draws below stay inside these ranges and needn't reach their ends.
All inputs are finite; a program needn't handle non-finite values.
Results may differ from the reference program's by a relative error of at most 0.0054.
Values may be sent and summed in bfloat16 or wider, within the bound.
No kernel may reach another device: no remote copies, remote signals or barrier semaphores. Data moves between devices by JAX's collectives and lax.ppermute only.
A program may use at most 64 MiB of HBM per device.

```python
import jax
import jax.numpy as jnp
from jax import lax

NAUX = 1024
NAO = 1024
NVIR = 512
OCC_DEV = 1
HOPS = 2
NOCC = 512
N_AUX = 16
N_OCC = 32


def block_scale(own_key, shape, cuts, least, top_value):
    gain, own = 1.0, jax.random.fold_in(own_key, 6)
    for axis_at, blocks in cuts:
        draws = jnp.exp(jax.random.uniform(jax.random.fold_in(own, axis_at), (blocks,), jnp.float32, least / len(cuts), top_value / len(cuts)))
        gain = gain * jnp.repeat(draws, shape[axis_at] // blocks).reshape([-1 if axis == axis_at else 1 for axis in range(len(shape))])
    return gain


def bell_draw(stream_key, extent, width, bound, cuts=(), kind=jnp.bfloat16):
    result = width * jax.random.normal(stream_key, extent, jnp.float32)
    if cuts:
        result = result * block_scale(stream_key, extent, cuts, -0.22, 0.18)
    return jnp.clip(result, -bound, bound).astype(kind)


def setup_inputs(seed: int = 0) -> dict:
    keys = jax.random.split(jax.random.key(seed), 5)
    half_ints = bell_draw(keys[0], (NAUX, NOCC, NAO), 0.12, 0.71875, ((0, 16), (1, 32)))
    orbitals = bell_draw(keys[1], (NAO, NVIR), NAO ** -0.5, 0.1875)
    eps_occ = jnp.clip(jax.random.uniform(keys[2], (NOCC,), jnp.float32, -1.5, -0.3), -1.5, -0.3)
    eps_vir = jnp.clip(jax.random.uniform(keys[3], (NVIR,), jnp.float32, 0.3, 2.5), 0.3, 2.5)
    return dict(half_ints=half_ints, orbitals=orbitals, eps_occ=eps_occ, eps_vir=eps_vir)


def pair_density(own_block, own_eps, partner, partner_eps, eps_vir):
    occ_dev = own_block.shape[1]
    nvir = own_block.shape[2]
    own_flat = own_block.astype(jnp.float32).reshape(-1, occ_dev * nvir)
    partner_flat = partner.astype(jnp.float32).reshape(-1, occ_dev * nvir)
    coulomb = jnp.dot(own_flat.T, partner_flat, preferred_element_type=jnp.float32)
    coulomb = coulomb.reshape(occ_dev, nvir, occ_dev, nvir)
    swapped = jnp.transpose(coulomb, (0, 3, 2, 1))
    denominator = own_eps[:, None, None, None] + partner_eps[None, None, :, None] - eps_vir[None, :, None, None] - eps_vir[None, None, None, :]
    amplitudes = ((2.0 * coulomb - swapped) / denominator).astype(jnp.bfloat16)
    amplitudes = amplitudes.astype(jnp.float32).reshape(occ_dev * nvir, occ_dev * nvir)
    return jnp.dot(partner_flat, amplitudes.T, preferred_element_type=jnp.float32)


def reference(half_ints, orbitals, eps_occ, eps_vir):
    group_size = OCC_DEV * N_AUX
    coeffs = orbitals.astype(jnp.float32)

    def transform(group_index):
        start = (group_index * group_size).astype(jnp.int32)
        piece = lax.dynamic_slice_in_dim(half_ints, start, group_size, 1).astype(jnp.float32)
        return jnp.einsum("pim,ma->pia", piece, coeffs).astype(jnp.bfloat16)

    transformed = lax.map(transform, jnp.arange(N_OCC, dtype=jnp.int32))
    transformed = transformed.reshape(N_OCC, NAUX, N_AUX, OCC_DEV, NVIR)

    def block_density(block_index):
        occ_group = block_index // N_AUX
        position = block_index % N_AUX
        own_block = transformed[occ_group][:, position]
        own_eps = lax.dynamic_slice_in_dim(eps_occ, (block_index * OCC_DEV).astype(jnp.int32), OCC_DEV)
        total = jnp.zeros((NAUX, OCC_DEV * NVIR), jnp.float32)
        for distance in range(HOPS + 1):
            other_group = (occ_group - distance) % N_OCC
            partner = transformed[other_group][:, position]
            start = ((other_group * N_AUX + position) * OCC_DEV).astype(jnp.int32)
            partner_eps = lax.dynamic_slice_in_dim(eps_occ, start, OCC_DEV)
            total = total + pair_density(own_block, own_eps, partner, partner_eps, eps_vir)
        return total.astype(jnp.bfloat16).reshape(NAUX, OCC_DEV, NVIR)

    blocks = lax.map(block_density, jnp.arange(N_OCC * N_AUX, dtype=jnp.int32))
    return jnp.transpose(blocks, (1, 0, 2, 3)).reshape(NAUX, NOCC, NVIR)
```

```python
import jax
import jax.numpy as jnp
import numpy as np
from jax import lax
from jax.sharding import Mesh, PartitionSpec as P

AXES = ("zh", "y", "c", "x", "zl")
SIZES = (2, 4, 2, 4, 8)
NEAR = 4
FIRST_N = ((0, 1), (2, 3))
FIRST_F = ((0, 1, 2, 3),)


def rank(zh, y, c, x, zl):
    return (((zh * 4 + y) * 2 + c) * 4 + x) * 8 + zl


def pairs_of(move):
    pairs = []
    for spot in np.ndindex(*SIZES):
        zh, y, c, x, zl = spot
        z, y2, c2, x2 = move(zh * 8 + zl, y, c, x)
        z, y2, x2 = z % 16, y2 % 4, x2 % 4
        pairs.append((rank(*spot), rank(z // 8, y2, c2, x2, z % 8)))
    return pairs


def near_out(dy):
    return pairs_of(lambda z, y, c, x: (z + NEAR, y + dy, c, x))


def near_back(dy):
    return pairs_of(lambda z, y, c, x: (z - NEAR, y - dy, c, x))


def far_out(dy):
    return pairs_of(lambda z, y, c, x: (z + NEAR - 6, y + dy, c, x + (1 if z % 8 >= 6 else 0)))


def far_back(dy):
    return pairs_of(lambda z, y, c, x: (z + 8 - NEAR, y - dy, c, x))


def onward(z, y, c, x):
    return z + 1, y, c, x + (1 if (z - NEAR) % 8 == 7 else 0)


def backward(z, y, c, x):
    return z - 1, y, c, x - (1 if (z - NEAR) % 8 == 0 else 0)


def across(z, y, c, x):
    return z, y, 1 - c, x


def send(value, pairs):
    return lax.ppermute(value, AXES, pairs)


def body(half_ints, orbitals, eps_occ, eps_vir):
    zh, y, c, x, zl = (lax.axis_index(name) for name in AXES)
    naux, group, nao = half_ints.shape
    nvir = orbitals.shape[1]
    near_set = zh ^ (x & 1)
    local = lax.dot_general(
        half_ints, orbitals, (((2,), (0,)), ((), ())), preferred_element_type=jnp.float32
    ).astype(jnp.bfloat16)
    local = jnp.transpose(local, (1, 0, 2))
    mine = lax.dynamic_slice_in_dim(local, c * 8, 8)
    other = send(lax.dynamic_slice_in_dim(local, (1 - c) * 8, 8), pairs_of(across))

    def piece(chain_set, dy):
        at = chain_set * 4 + (y + dy) % 4
        return jnp.concatenate(
            [lax.dynamic_slice_in_dim(mine, at, 1), lax.dynamic_slice_in_dim(other, at, 1)]
        ).reshape(2 * naux, nvir)

    n0 = [None] * 4
    f2 = [None] * 4
    for dy in range(4):
        n0[dy] = send(piece(near_set, dy), near_out(dy))
        f2[dy] = send(piece(1 - near_set, dy), far_out(dy))
    join = jnp.concatenate
    n0 = [join([n0[dy] for dy in part]) for part in FIRST_N]
    f2 = [join([f2[dy] for dy in part]) for part in FIRST_F]
    n1 = [send(part, pairs_of(onward)) for part in n0]
    f1 = [send(part, pairs_of(backward)) for part in f2]
    n2 = [send(part, pairs_of(onward)) for part in n1]
    f0 = [send(part, pairs_of(backward)) for part in f1]
    near = [join(part) for part in (n0, n1, n2)]
    far = [join(part) for part in (f0, f1, f2)]

    spot = (zh * 8 + zl - NEAR) % 16
    own_zl = spot % 8
    own_group = x * 8 + own_zl
    own_set = (spot // 8) ^ (x & 1)
    position = c * 8 + own_set * 4 + y

    def eps_at(distance):
        return eps_occ[((own_group - distance) % 32) * group + position]

    def cross(left, right):
        return lax.dot_general(left, right, (((0,), (0,)), ((), ())), preferred_element_type=jnp.float32)

    def spread(right, amps):
        return lax.dot_general(right, amps, (((1,), (1,)), ((), ())), preferred_element_type=jnp.float32)

    own_n, own_f = near[0], far[0]
    dens_n = dens_f = 0.0
    for distance in range(3):
        swap = own_zl < distance
        other_n = jnp.where(swap, far[distance], near[distance]) if distance else own_n
        other_f = jnp.where(swap, near[distance], far[distance]) if distance else own_f
        top = cross(own_n, other_n) + cross(own_f, other_f)
        if distance:
            top = 2.0 * top - (cross(other_n, own_n) + cross(other_f, own_f))
        amps = (
            top / (eps_at(0) + eps_at(distance) - eps_vir[:, None] - eps_vir[None, :])
        ).astype(jnp.bfloat16)
        dens_n = dens_n + spread(other_n, amps)
        dens_f = dens_f + spread(other_f, amps)
    dens_n = dens_n.astype(jnp.bfloat16).reshape(4, 2 * naux, nvir)
    dens_f = dens_f.astype(jnp.bfloat16).reshape(4, 2 * naux, nvir)

    back_n, back_f = [], []
    for dy in range(4):
        back_f.append(send(dens_f[dy], far_back(dy)))
        back_n.append(send(dens_n[dy], near_back(dy)))
    back_n = jnp.roll(jnp.stack(back_n), y, axis=0)
    back_f = jnp.roll(jnp.stack(back_f), y, axis=0)
    both = jnp.stack([back_n, back_f]).reshape(2, 4, 2, naux, nvir)
    both = jnp.where(near_set == 0, both, both[::-1])
    kept = both[:, :, 0].reshape(8, naux, nvir)
    given = send(both[:, :, 1].reshape(8, naux, nvir), pairs_of(across))
    full = join([jnp.where(c == 0, kept, given), jnp.where(c == 0, given, kept)])
    return jnp.transpose(full, (1, 0, 2))


def solution(mesh):
    fine = Mesh(mesh.devices.reshape(SIZES), AXES)
    placed = P(("zh", "y", "c"), ("x", "zl"), None)
    return jax.shard_map(
        body, mesh=fine, in_specs=(placed, P(), P(), P()), out_specs=placed, check_vma=False
    )
```

```python
import jax
import jax.numpy as jnp
import numpy as np
from jax import lax
from jax.sharding import Mesh, PartitionSpec as P

AXES = ("zh", "y", "c", "x", "zl")
SIZES = (2, 4, 2, 4, 8)
RING = ("zl", "zh")
PLANE = ("y", "c")
CHUNKS = (32, 32)


def rank(zh, y, c, x, zl):
    return (((zh * 4 + y) * 2 + c) * 4 + x) * 8 + zl


def next_group():
    pairs = []
    for zh, y, c, x, zl in np.ndindex(*SIZES):
        group = (x * 8 + y * 2 + c + 1) % 32
        pairs.append((rank(zh, y, c, x, zl), rank(zh, group // 2 % 4, group % 2, group // 8, zl)))
    return pairs


def exchange(value, axes):
    return lax.all_to_all(value, axes, split_axis=0, concat_axis=0, tiled=True)


def cross(left, right):
    return lax.dot_general(left, right, (((0,), (0,)), ((), ())), preferred_element_type=jnp.float32)


def spread(right, amps):
    return lax.dot_general(right, amps, (((1,), (1,)), ((), ())), preferred_element_type=jnp.float32)


def body(half_ints, orbitals, eps_occ, eps_vir):
    zh, y, c, x, zl = (lax.axis_index(name) for name in AXES)
    naux, group, nao = half_ints.shape
    nvir = orbitals.shape[1]
    local = lax.dot_general(
        half_ints, orbitals, (((2,), (0,)), ((), ())), preferred_element_type=jnp.float32
    ).astype(jnp.bfloat16)
    local = jnp.transpose(local, (1, 0, 2))

    start = 0
    parts = []
    for rows in CHUNKS:
        piece = local[:, start : start + rows]
        start += rows
        piece = exchange(piece, RING)
        piece = exchange(piece.reshape(8, 2 * rows, nvir), PLANE).reshape(16 * rows, nvir)
        first = lax.ppermute(piece, AXES, next_group())
        parts.append((piece, first, lax.ppermute(first, AXES, next_group())))

    own_group = x * 8 + y * 2 + c
    position = zl * 2 + zh

    def eps_at(distance):
        return eps_occ[((own_group - distance) % 32) * group + position]

    dens = [0.0] * len(parts)
    for distance in range(3):
        top = 0.0
        for part in parts:
            own, other = part[0], part[distance]
            if distance:
                top = top + (2.0 * cross(own, other) - cross(other, own))
            else:
                top = top + cross(own, own)
        amps = (
            top / (eps_at(0) + eps_at(distance) - eps_vir[:, None] - eps_vir[None, :])
        ).astype(jnp.bfloat16)
        dens = [done + spread(part[distance], amps) for done, part in zip(dens, parts)]

    out = []
    for rows, value in zip(CHUNKS, dens):
        value = exchange(value.astype(jnp.bfloat16).reshape(8, 2 * rows, nvir), PLANE)
        value = exchange(value.reshape(16, rows, nvir), RING)
        out.append(value)
    return jnp.concatenate([jnp.transpose(value, (1, 0, 2)) for value in out])


def solution(mesh):
    fine = Mesh(mesh.devices.reshape(SIZES), AXES)
    placed = P(("zh", "y", "c"), ("x", "zl"), None)
    return jax.shard_map(
        body, mesh=fine, in_specs=(placed, P(), P(), P()), out_specs=placed, check_vma=False
    )
```

```python
import jax
import jax.numpy as jnp
import numpy as np
from jax import lax
from jax.sharding import Mesh, PartitionSpec as P

AXES = ("zh", "y", "c", "x", "zl")
SIZES = (2, 4, 2, 4, 8)
NEAR = 3
CHUNKS = (32, 32)


def rank(zh, y, c, x, zl):
    return (((zh * 4 + y) * 2 + c) * 4 + x) * 8 + zl


def pairs_of(move):
    pairs = []
    for spot in np.ndindex(*SIZES):
        zh, y, c, x, zl = spot
        z, c2, x2 = move(zh * 8 + zl, c, x)
        z, x2 = z % 16, x2 % 4
        pairs.append((rank(*spot), rank(z // 8, y, c2, x2, z % 8)))
    return pairs


def outward(z, c, x):
    if c == z // 8 ^ x & 1:
        return z + NEAR, 0, x
    return z + NEAR - 6, 1, x + (1 if z % 8 >= 6 else 0)


def relay(z, c, x):
    if c == 0:
        return z + 1, c, x + (1 if (z - NEAR) % 8 == 7 else 0)
    return z - 1, c, x - (1 if (z - NEAR) % 8 == 0 else 0)


def homeward(z, c, x):
    owned = (z - NEAR) % 16 // 8 ^ x & 1
    return (z - NEAR if c == 0 else z + 8 - NEAR), owned, x


def across(z, c, x):
    return z, 1 - c, x


def send(value, move):
    return lax.ppermute(value, AXES, pairs_of(move))


def exchange(value):
    return lax.all_to_all(value, ("y", "c"), split_axis=0, concat_axis=0, tiled=True)


def cross(left, right):
    return lax.dot_general(left, right, (((0,), (0,)), ((), ())), preferred_element_type=jnp.float32)


def spread(right, amps):
    return lax.dot_general(right, amps, (((1,), (1,)), ((), ())), preferred_element_type=jnp.float32)


def body(half_ints, orbitals, eps_occ, eps_vir):
    zh, y, c, x, zl = (lax.axis_index(name) for name in AXES)
    naux, group, nao = half_ints.shape
    nvir = orbitals.shape[1]
    join = jnp.concatenate
    local = lax.dot_general(
        half_ints, orbitals, (((2,), (0,)), ((), ())), preferred_element_type=jnp.float32
    ).astype(jnp.bfloat16)
    local = jnp.transpose(local, (1, 0, 2))

    kept, got = ([], [], []), ([], [], [])
    start = 0
    for rows in CHUNKS:
        value = exchange(local[:, start : start + rows].reshape(8, 2, rows, nvir))
        start += rows
        for stage in range(3):
            value = send(value, relay if stage else outward)
            mine = lax.dynamic_index_in_dim(value, c, 1, keepdims=False)
            other = lax.dynamic_index_in_dim(value, 1 - c, 1, keepdims=False)
            kept[stage].append(mine.reshape(8 * rows, nvir))
            got[stage].append(send(other, across).reshape(8 * rows, nvir))
    kept = [join(parts) for parts in kept]
    got = [join(parts) for parts in got]

    spot = (zh * 8 + zl - NEAR) % 16
    own_zl = spot % 8
    own_group = x * 8 + own_zl
    position = y * 4 + ((spot // 8) ^ (x & 1)) * 2 + c

    def eps_at(distance):
        return eps_occ[((own_group - distance) % 32) * group + position]

    near, far = [], []
    for distance in range(3):
        near.append(jnp.where(c == 0, kept[distance], got[distance]))
        far.append(jnp.where(c == 0, got[2 - distance], kept[2 - distance]))
    own_n, own_f = near[0], far[0]
    dens_n = dens_f = 0.0
    for distance in range(3):
        swap = own_zl < distance
        other_n = jnp.where(swap, far[distance], near[distance]) if distance else own_n
        other_f = jnp.where(swap, near[distance], far[distance]) if distance else own_f
        top = cross(own_n, other_n) + cross(own_f, other_f)
        if distance:
            top = 2.0 * top - (cross(other_n, own_n) + cross(other_f, own_f))
        amps = (
            top / (eps_at(0) + eps_at(distance) - eps_vir[:, None] - eps_vir[None, :])
        ).astype(jnp.bfloat16)
        dens_n = dens_n + spread(other_n, amps)
        dens_f = dens_f + spread(other_f, amps)
    dens_n = dens_n.astype(jnp.bfloat16)
    dens_f = dens_f.astype(jnp.bfloat16)
    keep = jnp.where(c == 0, dens_n, dens_f)
    give = jnp.where(c == 0, dens_f, dens_n)

    out = []
    start = 0
    for rows in CHUNKS:
        part = slice(8 * start, 8 * (start + rows))
        start += rows
        mine = keep[part].reshape(8, rows, nvir)
        other = send(give[part], across).reshape(8, rows, nvir)
        value = jnp.stack([jnp.where(c == 0, mine, other), jnp.where(c == 0, other, mine)], axis=1)
        value = exchange(send(value, homeward)).reshape(group, rows, nvir)
        out.append(jnp.transpose(value, (1, 0, 2)))
    return join(out)


def solution(mesh):
    fine = Mesh(mesh.devices.reshape(SIZES), AXES)
    placed = P(("zh", "y", "c"), ("x", "zl"), None)
    return jax.shard_map(
        body, mesh=fine, in_specs=(placed, P(), P(), P()), out_specs=placed, check_vma=False
    )
```

```python
import jax
import jax.numpy as jnp
import numpy as np
from jax import lax
from jax.sharding import Mesh, PartitionSpec as P

AXES = ("zh", "y", "c", "x", "zl")
SIZES = (2, 4, 2, 4, 8)
NEAR = 3


def rank(zh, y, c, x, zl):
    return (((zh * 4 + y) * 2 + c) * 4 + x) * 8 + zl


def pairs_of(move):
    pairs = []
    for spot in np.ndindex(*SIZES):
        zh, y, c, x, zl = spot
        z, c2, x2 = move(zh * 8 + zl, c, x)
        z, x2 = z % 16, x2 % 4
        pairs.append((rank(*spot), rank(z // 8, y, c2, x2, z % 8)))
    return pairs


def outward(z, c, x):
    if c == z // 8 ^ x & 1:
        return z + NEAR, 0, x
    return z + NEAR - 6, 1, x + (1 if z % 8 >= 6 else 0)


def relay(z, c, x):
    if c == 0:
        return z + 1, c, x + (1 if (z - NEAR) % 8 == 7 else 0)
    return z - 1, c, x - (1 if (z - NEAR) % 8 == 0 else 0)


def homeward(z, c, x):
    owned = (z - NEAR) % 16 // 8 ^ x & 1
    return (z - NEAR if c == 0 else z + 8 - NEAR), owned, x


def across(z, c, x):
    return z, 1 - c, x


def send(value, move):
    return lax.ppermute(value, AXES, pairs_of(move))


def exchange(value):
    return lax.all_to_all(value, ("y", "c"), split_axis=0, concat_axis=0, tiled=True)


def after(value, other):
    return lax.optimization_barrier((value, other))[0]


def cross(left, right):
    return lax.dot_general(left, right, (((0,), (0,)), ((), ())), preferred_element_type=jnp.float32)


def spread(right, amps):
    return lax.dot_general(right, amps, (((1,), (1,)), ((), ())), preferred_element_type=jnp.float32)


def body(half_ints, orbitals, eps_occ, eps_vir):
    zh, y, c, x, zl = (lax.axis_index(name) for name in AXES)
    naux, group, nao = half_ints.shape
    nvir = orbitals.shape[1]
    local = lax.dot_general(
        half_ints, orbitals, (((2,), (0,)), ((), ())), preferred_element_type=jnp.float32
    ).astype(jnp.bfloat16)
    local = jnp.transpose(local, (1, 0, 2))

    spot = (zh * 8 + zl - NEAR) % 16
    own_zl = spot % 8
    own_group = x * 8 + own_zl
    row = y * 2 + ((spot // 8) ^ (x & 1))

    def density(mine, got, wave):
        def eps_at(distance):
            return eps_occ[((own_group - distance) % 32) * group + wave * 8 + row]

        mine = [value.reshape(8 * naux, nvir) for value in mine]
        got = [value.reshape(8 * naux, nvir) for value in got]
        first = c == 0
        own_m = jnp.where(first, mine[0], mine[2])
        own_o = jnp.where(first, got[2], got[0])
        total = 0.0
        for distance in range(3):
            other_m, other_o = own_m, own_o
            if distance:
                held = jnp.where(first, mine[distance], mine[2 - distance])
                met = jnp.where(first, got[2 - distance], got[distance])
                turned = own_zl < distance
                other_m = jnp.where(turned, met, held)
                other_o = jnp.where(turned, held, met)
            top = cross(own_m, other_m) + cross(own_o, other_o)
            if distance:
                top = 2.0 * top - (cross(other_m, own_m) + cross(other_o, own_o))
            amps = (
                top / (eps_at(0) + eps_at(distance) - eps_vir[:, None] - eps_vir[None, :])
            ).astype(jnp.bfloat16)
            total = total + spread(other_m, amps)
        return total.astype(jnp.bfloat16).reshape(8, naux, nvir)

    mine, got = ([], []), ([], [])
    for wave in range(2):
        mine[wave].append(send(exchange(local[wave * 8 : wave * 8 + 8]), outward))
    for stage in range(2):
        got[0].append(send(mine[0][stage], across))
        mine[0].append(send(mine[0][stage], relay))
        mine[1][stage] = after(mine[1][stage], got[0][stage])
        mine[1].append(send(mine[1][stage], relay))
        got[1].append(send(mine[1][stage], across))
    got[0].append(send(mine[0][2], across))
    done = density(mine[0], got[0], 0)
    back = [send(done, homeward)]
    mine[1][2] = after(mine[1][2], done)
    got[1].append(send(mine[1][2], across))
    back.append(send(density(mine[1], got[1], 1), homeward))
    out = [jnp.transpose(exchange(value), (1, 0, 2)) for value in back]
    return jnp.concatenate(out, axis=1)


def solution(mesh):
    fine = Mesh(mesh.devices.reshape(SIZES), AXES)
    placed = P(("zh", "y", "c"), ("x", "zl"), None)
    return jax.shard_map(
        body, mesh=fine, in_specs=(placed, P(), P(), P()), out_specs=placed, check_vma=False
    )
```

```python
import functools

import jax
import jax.numpy as jnp
import numpy as np
from jax import lax
from jax.experimental import pallas as pl
from jax.experimental.pallas import tpu as pltpu
from jax.sharding import Mesh, PartitionSpec as P

AXES = ("zh", "y", "c", "x", "zl")
SIZES = (2, 4, 2, 4, 8)
NEAR = 3


def rank(zh, y, c, x, zl):
    return (((zh * 4 + y) * 2 + c) * 4 + x) * 8 + zl


def pairs_of(move):
    pairs = []
    for spot in np.ndindex(*SIZES):
        zh, y, c, x, zl = spot
        z, c2, x2 = move(zh * 8 + zl, c, x)
        z, x2 = z % 16, x2 % 4
        pairs.append((rank(*spot), rank(z // 8, y, c2, x2, z % 8)))
    return pairs


def outward(z, c, x):
    if c == z // 8 ^ x & 1:
        return z + NEAR, 0, x
    return z + NEAR - 6, 1, x + (1 if z % 8 >= 6 else 0)


def relay(z, c, x):
    if c == 0:
        return z + 1, c, x + (1 if (z - NEAR) % 8 == 7 else 0)
    return z - 1, c, x - (1 if (z - NEAR) % 8 == 0 else 0)


def homeward(z, c, x):
    owned = (z - NEAR) % 16 // 8 ^ x & 1
    return (z - NEAR if c == 0 else z + 8 - NEAR), owned, x


def across(z, c, x):
    return z, 1 - c, x


def send(value, move):
    return lax.ppermute(value, AXES, pairs_of(move))


def exchange(value):
    return lax.all_to_all(value, ("y", "c"), split_axis=0, concat_axis=0, tiled=True)


def after(value, other):
    return lax.optimization_barrier((value, other))[0]


def cross(left, right):
    return lax.dot_general(left, right, (((0,), (0,)), ((), ())), preferred_element_type=jnp.float32)


def spread(right, amps):
    return lax.dot_general(right, amps, (((1,), (1,)), ((), ())), preferred_element_type=jnp.float32)


def pair_kernel(wave, eps, across_vir, down_vir, m0, m1, m2, g0, g1, g2, out, held, met):
    zh, y, c, x, zl = (lax.axis_index(name) for name in AXES)
    spot = (zh * 8 + zl + 16 - NEAR) & 15
    own_zl = spot & 7
    own_group = x * 8 + own_zl
    row = wave * 8 + y * 2 + ((spot // 8) ^ (x & 1))
    mine, got = (m0, m1, m2), (g0, g1, g2)
    for distance in range(3):
        first = mine[distance], mine[2 - distance]
        second = got[2 - distance], got[distance]
        for core in range(2):
            for turned in range(2 if distance else 1):
                here = c == core
                if distance:
                    here = jnp.logical_and(here, (own_zl < distance) == (turned == 1))

                @pl.when(here)
                def _(a=first[core], b=second[core], turned=turned, distance=distance):
                    held[distance] = (b if turned else a)[...]
                    met[distance] = (a if turned else b)[...]

    own = eps[own_group * 16 + row]
    total = None
    for distance in range(3):
        gap = own + eps[((own_group + 32 - distance) & 31) * 16 + row]
        top = cross(held[0], held[distance]) + cross(met[0], met[distance])
        if distance:
            turn = cross(held[distance], held[0]) + cross(met[distance], met[0])
            top = 2.0 * top - turn
        amps = (top / (gap - down_vir[...] - across_vir[...])).astype(jnp.bfloat16)
        part = spread(held[distance], amps)
        total = part if total is None else total + part
    out[...] = total.astype(jnp.bfloat16)


def density(wave, eps_occ, across_vir, down_vir, mine, got):
    rows, nvir = mine[0].shape
    vmem = pl.BlockSpec(memory_space=pltpu.VMEM)
    return pl.pallas_call(
        functools.partial(pair_kernel, wave),
        out_shape=jax.ShapeDtypeStruct((rows, nvir), jnp.bfloat16),
        in_specs=[pl.BlockSpec(memory_space=pltpu.SMEM)] + [vmem] * 8,
        out_specs=vmem,
        scratch_shapes=[pltpu.VMEM((3, rows, nvir), jnp.bfloat16)] * 2,
        cost_estimate=pl.CostEstimate(
            flops=26 * rows * nvir * nvir, bytes_accessed=14 * rows * nvir, transcendentals=0
        ),
        name="pair_stage",
    )(eps_occ, across_vir, down_vir, *mine, *got)


def body(half_ints, orbitals, eps_occ, eps_vir):
    naux, group, nao = half_ints.shape
    nvir = orbitals.shape[1]
    local = lax.dot_general(
        half_ints, orbitals, (((2,), (0,)), ((), ())), preferred_element_type=jnp.float32
    ).astype(jnp.bfloat16)
    local = jnp.transpose(local, (1, 0, 2))
    across_vir, down_vir = eps_vir.reshape(1, nvir), eps_vir.reshape(nvir, 1)

    mine, got = ([], []), ([], [])
    pieces = [exchange(local[wave * 8 : wave * 8 + 8]).reshape(8 * naux, nvir) for wave in range(2)]
    for wave in range(2):
        mine[wave].append(send(pieces[wave], outward))
    mine[0][0] = after(mine[0][0], pieces[1])
    for stage in range(2):
        got[0].append(send(mine[0][stage], across))
        mine[0].append(send(mine[0][stage], relay))
        mine[1][stage] = after(mine[1][stage], got[0][stage])
        mine[1].append(send(mine[1][stage], relay))
        got[1].append(send(mine[1][stage], across))
    got[0].append(send(mine[0][2], across))
    done = density(0, eps_occ, across_vir, down_vir, mine[0], got[0])
    back = [send(done, homeward)]
    mine[1][2] = after(mine[1][2], done)
    got[1].append(send(mine[1][2], across))
    done = density(1, eps_occ, across_vir, down_vir, mine[1], got[1])
    back.append(send(done, homeward))
    out = [exchange(value.reshape(8, naux, nvir)) for value in back]
    return jnp.concatenate([jnp.transpose(value, (1, 0, 2)) for value in out], axis=1)


def solution(mesh):
    fine = Mesh(mesh.devices.reshape(SIZES), AXES)
    placed = P(("zh", "y", "c"), ("x", "zl"), None)
    return jax.shard_map(
        body, mesh=fine, in_specs=(placed, P(), P(), P()), out_specs=placed, check_vma=False
    )
```

```python
import functools

import jax
import jax.numpy as jnp
import numpy as np
from jax import lax
from jax.experimental import pallas as pl
from jax.experimental.pallas import tpu as pltpu
from jax.sharding import Mesh, PartitionSpec as P

AXES = ("zh", "y", "c", "x", "zl")
SIZES = (2, 4, 2, 4, 8)
NEAR = 4


def rank(zh, y, c, x, zl):
    return (((zh * 4 + y) * 2 + c) * 4 + x) * 8 + zl


def pairs_of(move):
    pairs = []
    for spot in np.ndindex(*SIZES):
        zh, y, c, x, zl = spot
        z, c2, x2 = move(zh * 8 + zl, c, x)
        z, x2 = z % 16, x2 % 4
        pairs.append((rank(*spot), rank(z // 8, y, c2, x2, z % 8)))
    return pairs


def outward(z, c, x):
    if c == z // 8 ^ x & 1:
        return z + NEAR, 0, x
    return z + NEAR - 6, 1, x + (1 if z % 8 >= 6 else 0)


def relay(z, c, x):
    if c == 0:
        return z + 1, c, x + (1 if (z - NEAR) % 8 == 7 else 0)
    return z - 1, c, x - (1 if (z - NEAR) % 8 == 0 else 0)


def homeward(z, c, x):
    owned = (z - NEAR) % 16 // 8 ^ x & 1
    return (z - NEAR if c == 0 else z + 8 - NEAR), owned, x


def across(z, c, x):
    return z, 1 - c, x


def send(value, move):
    return lax.ppermute(value, AXES, pairs_of(move))


def exchange(value):
    return lax.all_to_all(value, ("y", "c"), split_axis=0, concat_axis=0, tiled=True)


def after(value, other):
    return lax.optimization_barrier((value, other))[0]


def cross(left, right):
    return lax.dot_general(left, right, (((0,), (0,)), ((), ())), preferred_element_type=jnp.float32)


def spread(right, amps):
    return lax.dot_general(right, amps, (((1,), (1,)), ((), ())), preferred_element_type=jnp.float32)


def pair_kernel(wave, eps, across_vir, down_vir, m0, m1, m2, g0, g1, g2, out, held, met):
    zh, y, c, x, zl = (lax.axis_index(name) for name in AXES)
    spot = (zh * 8 + zl + 16 - NEAR) & 15
    own_zl = spot & 7
    own_group = x * 8 + own_zl
    row = wave * 8 + y * 2 + ((spot // 8) ^ (x & 1))
    mine, got = (m0, m1, m2), (g0, g1, g2)
    for distance in range(3):
        first = mine[distance], mine[2 - distance]
        second = got[2 - distance], got[distance]
        for core in range(2):
            for turned in range(2 if distance else 1):
                here = c == core
                if distance:
                    here = jnp.logical_and(here, (own_zl < distance) == (turned == 1))

                @pl.when(here)
                def _(a=first[core], b=second[core], turned=turned, distance=distance):
                    held[distance] = (b if turned else a)[...]
                    met[distance] = (a if turned else b)[...]

    own = eps[own_group * 16 + row]
    total = None
    for distance in range(3):
        gap = own + eps[((own_group + 32 - distance) & 31) * 16 + row]
        top = cross(held[0], held[distance]) + cross(met[0], met[distance])
        if distance:
            turn = cross(held[distance], held[0]) + cross(met[distance], met[0])
            top = 2.0 * top - turn
        amps = (top / (gap - down_vir[...] - across_vir[...])).astype(jnp.bfloat16)
        part = spread(held[distance], amps)
        total = part if total is None else total + part
    out[...] = total.astype(jnp.bfloat16)


def density(wave, eps_occ, across_vir, down_vir, mine, got):
    rows, nvir = mine[0].shape
    vmem = pl.BlockSpec(memory_space=pltpu.VMEM)
    return pl.pallas_call(
        functools.partial(pair_kernel, wave),
        out_shape=jax.ShapeDtypeStruct((rows, nvir), jnp.bfloat16),
        in_specs=[pl.BlockSpec(memory_space=pltpu.SMEM)] + [vmem] * 8,
        out_specs=vmem,
        scratch_shapes=[pltpu.VMEM((3, rows, nvir), jnp.bfloat16)] * 2,
        cost_estimate=pl.CostEstimate(
            flops=26 * rows * nvir * nvir, bytes_accessed=14 * rows * nvir, transcendentals=0
        ),
        name="pair_stage",
    )(eps_occ, across_vir, down_vir, *mine, *got)


def body(half_ints, orbitals, eps_occ, eps_vir):
    naux, _, _ = half_ints.shape
    nvir = orbitals.shape[1]
    local = lax.dot_general(
        half_ints, orbitals, (((2,), (0,)), ((), ())), preferred_element_type=jnp.float32
    ).astype(jnp.bfloat16)
    local = jnp.transpose(local, (1, 0, 2))
    across_vir, down_vir = eps_vir.reshape(1, nvir), eps_vir.reshape(nvir, 1)

    mine, got = ([], []), ([], [])
    pieces = [exchange(local[wave * 8 : wave * 8 + 8]).reshape(8 * naux, nvir) for wave in range(2)]
    for wave in range(2):
        mine[wave].append(send(pieces[wave], outward))
    mine[0][0] = after(mine[0][0], pieces[1])
    down_vir = after(down_vir, pieces[1])
    for stage in range(2):
        got[0].append(send(mine[0][stage], across))
        mine[0].append(send(mine[0][stage], relay))
        mine[1][stage] = after(mine[1][stage], [got[0][stage], down_vir, *got[1]])
        mine[1].append(send(mine[1][stage], relay))
        if stage == 0:
            got[1].append(send(mine[1][0], across))
    got[0].append(send(mine[0][2], across))
    done = density(0, eps_occ, across_vir, down_vir, mine[0], got[0])
    back = [send(done, homeward)]
    for stage in (1, 2):
        mine[1][stage] = after(mine[1][stage], done)
        got[1].append(send(mine[1][stage], across))
    done = density(1, eps_occ, across_vir, down_vir, mine[1], got[1])
    back.append(send(done, homeward))
    out = [exchange(value.reshape(8, naux, nvir)) for value in back]
    return jnp.concatenate([jnp.transpose(value, (1, 0, 2)) for value in out], axis=1)


def solution(mesh):
    fine = Mesh(mesh.devices.reshape(SIZES), AXES)
    placed = P(("zh", "y", "c"), ("x", "zl"), None)

    return jax.shard_map(
        body, mesh=fine, in_specs=(placed, P(), P(), P()), out_specs=placed, check_vma=False
    )
```

```python
import functools

import jax
import jax.numpy as jnp
import numpy as np
from jax import lax
from jax.experimental import pallas as pl
from jax.experimental.pallas import tpu as pltpu
from jax.sharding import Mesh, PartitionSpec as P

AXES = ("zh", "y", "c", "x", "zl")
SIZES = (2, 4, 2, 4, 8)
NEAR = (3, 3)


def rank(zh, y, c, x, zl):
    return (((zh * 4 + y) * 2 + c) * 4 + x) * 8 + zl


def pairs_of(move, near):
    pairs = []
    for spot in np.ndindex(*SIZES):
        zh, y, c, x, zl = spot
        z, c2, x2 = move(zh * 8 + zl, c, x, near)
        z, x2 = z % 16, x2 % 4
        pairs.append((rank(*spot), rank(z // 8, y, c2, x2, z % 8)))
    return pairs


def outward(z, c, x, near):
    if c == z // 8 ^ x & 1:
        return z + near, 0, x
    return z + near - 6, 1, x + (1 if z % 8 >= 6 else 0)


def relay(z, c, x, near):
    if c == 0:
        return z + 1, c, x + (1 if (z - near) % 8 == 7 else 0)
    return z - 1, c, x - (1 if (z - near) % 8 == 0 else 0)


def homeward(z, c, x, near):
    owned = (z - near) % 16 // 8 ^ x & 1
    return (z - near if c == 0 else z + 8 - near), owned, x


def across(z, c, x, near):
    return z, 1 - c, x


def send(value, move, wave):
    return lax.ppermute(value, AXES, pairs_of(move, NEAR[wave]))


def exchange(value):
    return lax.all_to_all(value, ("y", "c"), split_axis=0, concat_axis=0, tiled=True)


def after(value, other):
    return lax.optimization_barrier((value, other))[0]


def cross(left, right):
    return lax.dot_general(left, right, (((0,), (0,)), ((), ())), preferred_element_type=jnp.float32)


def spread(right, amps):
    return lax.dot_general(right, amps, (((1,), (1,)), ((), ())), preferred_element_type=jnp.float32)


def pair_kernel(wave, eps, across_vir, m0, m1, m2, g0, g1, g2, out, held, met):
    zh, y, c, x, zl = (lax.axis_index(name) for name in AXES)
    spot = (zh * 8 + zl + 16 - NEAR[wave]) & 15
    own_zl = spot & 7
    own_group = x * 8 + own_zl
    row = wave * 8 + y * 2 + ((spot // 8) ^ (x & 1))
    mine, got = (m0, m1, m2), (g0, g1, g2)
    for distance in range(3):
        first = mine[distance], mine[2 - distance]
        second = got[2 - distance], got[distance]
        for core in range(2):
            for turned in range(2 if distance else 1):
                here = c == core
                if distance:
                    here = jnp.logical_and(here, (own_zl < distance) == (turned == 1))

                @pl.when(here)
                def _(a=first[core], b=second[core], turned=turned, distance=distance):
                    held[distance] = (b if turned else a)[...]
                    met[distance] = (a if turned else b)[...]

    own = eps[own_group * 16 + row]
    down_vir = jnp.transpose(jnp.broadcast_to(across_vir[...], (128, out.shape[1])))[:, :1]
    total = None
    for distance in range(3):
        gap = own + eps[((own_group + 32 - distance) & 31) * 16 + row]
        top = cross(held[0], held[distance]) + cross(met[0], met[distance])
        if distance:
            turn = cross(held[distance], held[0]) + cross(met[distance], met[0])
            top = 2.0 * top - turn
        amps = (top / (gap - down_vir - across_vir[...])).astype(jnp.bfloat16)
        part = spread(held[distance], amps)
        total = part if total is None else total + part
    out[...] = total.astype(jnp.bfloat16)


def density(wave, eps_occ, across_vir, mine, got):
    rows, nvir = mine[0].shape
    vmem = pl.BlockSpec(memory_space=pltpu.VMEM)
    return pl.pallas_call(
        functools.partial(pair_kernel, wave),
        out_shape=jax.ShapeDtypeStruct((rows, nvir), jnp.bfloat16),
        in_specs=[pl.BlockSpec(memory_space=pltpu.SMEM)] + [vmem] * 7,
        out_specs=vmem,
        scratch_shapes=[pltpu.VMEM((3, rows, nvir), jnp.bfloat16)] * 2,
        cost_estimate=pl.CostEstimate(
            flops=26 * rows * nvir * nvir, bytes_accessed=14 * rows * nvir, transcendentals=0
        ),
        compiler_params=pltpu.CompilerParams(vmem_limit_bytes=20 * 2**20),
        name="pair_stage",
    )(eps_occ, across_vir, *mine, *got)


def body(half_ints, orbitals, eps_occ, eps_vir):
    naux, _, _ = half_ints.shape
    nvir = orbitals.shape[1]
    local = lax.dot_general(
        half_ints, orbitals, (((2,), (0,)), ((), ())), preferred_element_type=jnp.float32
    ).astype(jnp.bfloat16)
    local = jnp.transpose(local, (1, 0, 2))
    across_vir = eps_vir.reshape(1, nvir)

    mine, got = ([], []), ([], [])
    pieces = [exchange(local[wave * 8 : wave * 8 + 8]).reshape(8 * naux, nvir) for wave in range(2)]
    for wave in range(2):
        mine[wave].append(send(pieces[wave], outward, wave))
    mine[0][0] = after(mine[0][0], pieces[1])
    for stage in range(2):
        got[0].append(send(mine[0][stage], across, 0))
        mine[0].append(send(mine[0][stage], relay, 0))
        mine[1][stage] = after(mine[1][stage], [got[0][stage], *got[1]])
        mine[1].append(send(mine[1][stage], relay, 1))
        if stage == 0:
            got[1].append(send(mine[1][0], across, 1))
    got[0].append(send(mine[0][2], across, 0))
    done = density(0, eps_occ, across_vir, mine[0], got[0])
    back = [send(done, homeward, 0)]
    for stage in (1, 2):
        mine[1][stage] = after(mine[1][stage], done)
        got[1].append(send(mine[1][stage], across, 1))
    done = density(1, eps_occ, across_vir, mine[1], got[1])
    back.append(send(done, homeward, 1))
    out = [exchange(value.reshape(8, naux, nvir)) for value in back]
    return jnp.concatenate([jnp.transpose(value, (1, 0, 2)) for value in out], axis=1)


def solution(mesh):
    fine = Mesh(mesh.devices.reshape(SIZES), AXES)
    placed = P(("zh", "y", "c"), ("x", "zl"), None)

    return jax.shard_map(
        body, mesh=fine, in_specs=(placed, P(), P(), P()), out_specs=placed, check_vma=False
    )
```

```python
import functools

import jax
import jax.numpy as jnp
import numpy as np
from jax import lax
from jax.experimental import pallas as pl
from jax.experimental.pallas import tpu as pltpu
from jax.sharding import Mesh, PartitionSpec as P

AXES = ("zh", "y", "c", "x", "zl")
SIZES = (2, 4, 2, 4, 8)
NEAR = (3, 3)


def rank(zh, y, c, x, zl):
    return (((zh * 4 + y) * 2 + c) * 4 + x) * 8 + zl


def pairs_of(move, near):
    pairs = []
    for spot in np.ndindex(*SIZES):
        zh, y, c, x, zl = spot
        z, c2, x2 = move(zh * 8 + zl, c, x, near)
        z, x2 = z % 16, x2 % 4
        pairs.append((rank(*spot), rank(z // 8, y, c2, x2, z % 8)))
    return pairs


def outward(z, c, x, near):
    if c == z // 8 ^ x & 1:
        return z + near, 0, x
    return z + near - 6, 1, x + (1 if z % 8 >= 6 else 0)


def relay(z, c, x, near):
    if c == 0:
        return z + 1, c, x + (1 if (z - near) % 8 == 7 else 0)
    return z - 1, c, x - (1 if (z - near) % 8 == 0 else 0)


def homeward(z, c, x, near):
    owned = (z - near) % 16 // 8 ^ x & 1
    return (z - near if c == 0 else z + 8 - near), owned, x


def across(z, c, x, near):
    return z, 1 - c, x


def send(value, move, wave):
    return lax.ppermute(value, AXES, pairs_of(move, NEAR[wave]))


def exchange(value):
    return lax.all_to_all(value, ("y", "c"), split_axis=0, concat_axis=0, tiled=True)


def after(value, other):
    return lax.optimization_barrier((value, other))[0]


def cross(left, right):
    return lax.dot_general(left, right, (((0,), (0,)), ((), ())), preferred_element_type=jnp.float32)


def spread(right, amps):
    return lax.dot_general(right, amps, (((1,), (1,)), ((), ())), preferred_element_type=jnp.float32)


def pair_kernel(wave, eps, across_vir, m0, m1, m2, g0, g1, g2, out, held, met):
    zh, y, c, x, zl = (lax.axis_index(name) for name in AXES)
    spot = (zh * 8 + zl + 16 - NEAR[wave]) & 15
    own_zl = spot & 7
    own_group = x * 8 + own_zl
    row = wave * 8 + y * 2 + ((spot // 8) ^ (x & 1))
    mine, got = (m0, m1, m2), (g0, g1, g2)
    for distance in range(3):
        first = mine[distance], mine[2 - distance]
        second = got[2 - distance], got[distance]
        for core in range(2):
            for turned in range(2 if distance else 1):
                here = c == core
                if distance:
                    here = jnp.logical_and(here, (own_zl < distance) == (turned == 1))

                @pl.when(here)
                def _(a=first[core], b=second[core], turned=turned, distance=distance):
                    held[distance] = (b if turned else a)[...]
                    met[distance] = (a if turned else b)[...]

    own = eps[own_group * 16 + row]
    down_vir = jnp.transpose(jnp.broadcast_to(across_vir[...], (128, out.shape[1])))[:, :1]
    total = None
    for distance in range(3):
        gap = own + eps[((own_group + 32 - distance) & 31) * 16 + row]
        top = cross(held[0], held[distance]) + cross(met[0], met[distance])
        if distance:
            turn = cross(held[distance], held[0]) + cross(met[distance], met[0])
            top = 2.0 * top - turn
        amps = (top / (gap - down_vir - across_vir[...])).astype(jnp.bfloat16)
        part = spread(held[distance], amps)
        total = part if total is None else total + part
    out[...] = total.astype(jnp.bfloat16)


def density(wave, eps_occ, across_vir, mine, got):
    rows, nvir = mine[0].shape
    vmem = pl.BlockSpec(memory_space=pltpu.VMEM)
    return pl.pallas_call(
        functools.partial(pair_kernel, wave),
        out_shape=jax.ShapeDtypeStruct((rows, nvir), jnp.bfloat16),
        in_specs=[pl.BlockSpec(memory_space=pltpu.SMEM)] + [vmem] * 7,
        out_specs=vmem,
        scratch_shapes=[pltpu.VMEM((3, rows, nvir), jnp.bfloat16)] * 2,
        cost_estimate=pl.CostEstimate(
            flops=26 * rows * nvir * nvir, bytes_accessed=14 * rows * nvir, transcendentals=0
        ),
        compiler_params=pltpu.CompilerParams(vmem_limit_bytes=20 * 2**20),
        name="pair_stage",
    )(eps_occ, across_vir, *mine, *got)


def body(half_ints, orbitals, eps_occ, eps_vir):
    naux, _, _ = half_ints.shape
    nvir = orbitals.shape[1]
    local = lax.dot_general(
        half_ints, orbitals, (((2,), (0,)), ((), ())), preferred_element_type=jnp.float32
    ).astype(jnp.bfloat16)
    local = jnp.transpose(local, (1, 0, 2))
    across_vir = eps_vir.reshape(1, nvir)

    mine, got = ([], []), ([], [])
    pieces = [exchange(local[wave * 8 : wave * 8 + 8]).reshape(8 * naux, nvir) for wave in range(2)]
    for wave in range(2):
        mine[wave].append(send(pieces[wave], outward, wave))
    mine[0][0] = after(mine[0][0], pieces[1])
    for stage in range(2):
        got[0].append(send(mine[0][stage], across, 0))
        mine[0].append(send(mine[0][stage], relay, 0))
        if stage == 0:
            mine[1][0] = after(mine[1][0], got[0][0])
            mine[1].append(send(mine[1][0], relay, 1))
            got[1].append(send(mine[1][0], across, 1))
    got[0].append(send(mine[0][2], across, 0))
    done = density(0, eps_occ, across_vir, mine[0], got[0])
    back = [send(done, homeward, 0)]
    mine[1][1] = after(mine[1][1], [done, got[1][0]])
    mine[1].append(send(mine[1][1], relay, 1))
    got[1].append(send(mine[1][1], across, 1))
    mine[1][2] = after(mine[1][2], got[1][1])
    got[1].append(send(mine[1][2], across, 1))
    done = density(1, eps_occ, across_vir, mine[1], got[1])
    back.append(send(done, homeward, 1))
    out = [exchange(value.reshape(8, naux, nvir)) for value in back]
    return jnp.concatenate([jnp.transpose(value, (1, 0, 2)) for value in out], axis=1)


def solution(mesh):
    fine = Mesh(mesh.devices.reshape(SIZES), AXES)
    placed = P(("zh", "y", "c"), ("x", "zl"), None)

    return jax.shard_map(
        body, mesh=fine, in_specs=(placed, P(), P(), P()), out_specs=placed, check_vma=False
    )
```

```python
import functools

import jax
import jax.numpy as jnp
import numpy as np
from jax import lax
from jax.experimental import pallas as pl
from jax.experimental.pallas import tpu as pltpu
from jax.sharding import Mesh, PartitionSpec as P

AXES = ("zh", "y", "c", "x", "zl")
SIZES = (2, 4, 2, 4, 8)
NEAR = (3, 3)


def rank(zh, y, c, x, zl):
    return (((zh * 4 + y) * 2 + c) * 4 + x) * 8 + zl


def pairs_of(move, near):
    pairs = []
    for spot in np.ndindex(*SIZES):
        zh, y, c, x, zl = spot
        z, c2, x2 = move(zh * 8 + zl, c, x, near)
        z, x2 = z % 16, x2 % 4
        pairs.append((rank(*spot), rank(z // 8, y, c2, x2, z % 8)))
    return pairs


def outward(z, c, x, near):
    if c == z // 8 ^ x & 1:
        return z + near, 0, x
    return z + near - 6, 1, x + (1 if z % 8 >= 6 else 0)


def relay(z, c, x, near):
    if c == 0:
        return z + 1, c, x + (1 if (z - near) % 8 == 7 else 0)
    return z - 1, c, x - (1 if (z - near) % 8 == 0 else 0)


def homeward(z, c, x, near):
    owned = (z - near) % 16 // 8 ^ x & 1
    return (z - near if c == 0 else z + 8 - near), owned, x


def across(z, c, x, near):
    return z, 1 - c, x


def send(value, move, wave):
    return lax.ppermute(value, AXES, pairs_of(move, NEAR[wave]))


def exchange(value):
    return lax.all_to_all(value, ("y", "c"), split_axis=0, concat_axis=0, tiled=True)


def after(value, other):
    return lax.optimization_barrier((value, other))[0]


def cross(left, right):
    return lax.dot_general(left, right, (((0,), (0,)), ((), ())), preferred_element_type=jnp.float32)


def spread(right, amps):
    return lax.dot_general(right, amps, (((1,), (1,)), ((), ())), preferred_element_type=jnp.float32)


def pair_kernel(wave, eps, across_vir, m0, m1, m2, g0, g1, g2, out, held, met):
    zh, y, c, x, zl = (lax.axis_index(name) for name in AXES)
    spot = (zh * 8 + zl + 16 - NEAR[wave]) & 15
    own_zl = spot & 7
    own_group = x * 8 + own_zl
    row = wave * 8 + y * 2 + ((spot // 8) ^ (x & 1))
    mine, got = (m0, m1, m2), (g0, g1, g2)
    for distance in range(3):
        first = mine[distance], mine[2 - distance]
        second = got[2 - distance], got[distance]
        for core in range(2):
            for turned in range(2 if distance else 1):
                here = c == core
                if distance:
                    here = jnp.logical_and(here, (own_zl < distance) == (turned == 1))

                @pl.when(here)
                def _(a=first[core], b=second[core], turned=turned, distance=distance):
                    held[distance] = (b if turned else a)[...]
                    met[distance] = (a if turned else b)[...]

    own = eps[own_group * 16 + row]
    down_vir = jnp.transpose(jnp.broadcast_to(across_vir[...], (128, out.shape[1])))[:, :1]
    total = None
    for distance in range(3):
        gap = own + eps[((own_group + 32 - distance) & 31) * 16 + row]
        top = cross(held[0], held[distance]) + cross(met[0], met[distance])
        if distance:
            turn = cross(held[distance], held[0]) + cross(met[distance], met[0])
            top = 2.0 * top - turn
        amps = (top / (gap - down_vir - across_vir[...])).astype(jnp.bfloat16)
        part = spread(held[distance], amps)
        total = part if total is None else total + part
    out[...] = total.astype(jnp.bfloat16)


def density(wave, eps_occ, across_vir, mine, got):
    rows, nvir = mine[0].shape
    vmem = pl.BlockSpec(memory_space=pltpu.VMEM)
    return pl.pallas_call(
        functools.partial(pair_kernel, wave),
        out_shape=jax.ShapeDtypeStruct((rows, nvir), jnp.bfloat16),
        in_specs=[pl.BlockSpec(memory_space=pltpu.SMEM)] + [vmem] * 7,
        out_specs=vmem,
        scratch_shapes=[pltpu.VMEM((3, rows, nvir), jnp.bfloat16)] * 2,
        cost_estimate=pl.CostEstimate(
            flops=26 * rows * nvir * nvir, bytes_accessed=14 * rows * nvir, transcendentals=0
        ),
        compiler_params=pltpu.CompilerParams(vmem_limit_bytes=20 * 2**20),
        name="pair_stage",
    )(eps_occ, across_vir, *mine, *got)


def transform_kernel(ints, orbitals, out):
    rows, half, nao = ints.shape
    full = jnp.dot(
        ints[...].reshape(rows * half, nao), orbitals[...], preferred_element_type=jnp.float32
    )
    out[...] = jnp.transpose(full.reshape(rows, half, -1), (1, 0, 2)).astype(jnp.bfloat16)


def transform(wave, half_ints, orbitals):
    naux, group, nao = half_ints.shape
    nvir = orbitals.shape[1]
    half = group // 2
    return pl.pallas_call(
        transform_kernel,
        grid=(1,),
        out_shape=jax.ShapeDtypeStruct((half, naux, nvir), jnp.bfloat16),
        in_specs=[
            pl.BlockSpec((naux, half, nao), lambda i: (0, wave, 0)),
            pl.BlockSpec((nao, nvir), lambda i: (0, 0)),
        ],
        out_specs=pl.BlockSpec((half, naux, nvir), lambda i: (0, 0, 0)),
        cost_estimate=pl.CostEstimate(
            flops=2 * half * naux * nao * nvir,
            bytes_accessed=2 * (half * naux * (nao + nvir) + nao * nvir),
            transcendentals=0,
        ),
        name="transform",
    )(half_ints, orbitals)


def body(half_ints, orbitals, eps_occ, eps_vir):
    naux, _, _ = half_ints.shape
    nvir = orbitals.shape[1]
    across_vir = eps_vir.reshape(1, nvir)

    mine, got = ([], []), ([], [])
    local = [transform(wave, half_ints, orbitals) for wave in range(2)]
    pieces = [exchange(value).reshape(8 * naux, nvir) for value in local]
    for wave in range(2):
        mine[wave].append(send(pieces[wave], outward, wave))
    mine[0][0] = after(mine[0][0], pieces[1])
    for stage in range(2):
        got[0].append(send(mine[0][stage], across, 0))
        mine[0].append(send(mine[0][stage], relay, 0))
        mine[1][stage] = after(mine[1][stage], [got[0][stage], *got[1]])
        mine[1].append(send(mine[1][stage], relay, 1))
        if stage == 0:
            got[1].append(send(mine[1][0], across, 1))
    got[0].append(send(mine[0][2], across, 0))
    done = density(0, eps_occ, across_vir, mine[0], got[0])
    back = [send(done, homeward, 0)]
    for stage in (1, 2):
        mine[1][stage] = after(mine[1][stage], done)
        got[1].append(send(mine[1][stage], across, 1))
    done = density(1, eps_occ, across_vir, mine[1], got[1])
    back.append(send(done, homeward, 1))
    out = [exchange(value.reshape(8, naux, nvir)) for value in back]
    return jnp.concatenate([jnp.transpose(value, (1, 0, 2)) for value in out], axis=1)


def solution(mesh):
    fine = Mesh(mesh.devices.reshape(SIZES), AXES)
    placed = P(("zh", "y", "c"), ("x", "zl"), None)

    return jax.shard_map(
        body, mesh=fine, in_specs=(placed, P(), P(), P()), out_specs=placed, check_vma=False
    )
```
